32 devices in a mesh: gx: 2 (over x), yz: 16 (over z, y, core).
Axes of the slice: x: 2, y: 2, z: 4, core: 2. Of those that a mesh axis runs over, the one named last changes fastest.
Arguments:
- displacement: float32 [3, 8, 16, 8, 256], P(None, 'gx', 'yz'), may hold values from -0.04 to 0.04
- velocity: float32 [3, 8, 16, 8, 256], P(None, 'gx', 'yz'), may hold values from -5 to 5
- rest_length: float32 [18, 8, 16, 8, 256], P(None, 'gx', 'yz'), may hold values from 0.96 to 1.48, as said below
- heights: int32 [8, 32], replicated, may hold values from 512 to 1024
Outputs:
- new_displacement: float32 [3, 8, 16, 8, 256], P(None, 'gx', 'yz')
- half_velocity: float32 [3, 8, 16, 8, 256], P(None, 'gx', 'yz')
- boost_factor: float32 [], replicated
The draws below stay inside these ranges and needn't reach their ends.
Inputs may be any that keep to these rules, and one draw needn't show every extreme that they name: rest_length[k + 9] of an atom equals rest_length[k] of the atom -d_k away from it, wherever both atoms lie within the layers.
All inputs are finite; a program needn't handle non-finite values.
Results may differ from the reference program's by a relative error of at most 0.0003.
Values sent between devices are 32-bit elements; how exact they have to be, the bound alone decides.
A program may use at most 128 MiB of HBM per device.

```python
import jax
import jax.numpy as jnp
from jax import lax

CY = 8
CZ = 256
ZT = 4
YT = 4
TILES = 16
NX = 8
NY = 32
Z = 1024


def forward_bonds():
    chosen = []
    for along_x in (-1, 0, 1):
        for along_y in (-1, 0, 1):
            for along_z in (-1, 0, 1):
                length_sq = along_x * along_x + along_y * along_y + along_z * along_z
                if 0 < length_sq <= 2 and (along_x, along_y, along_z) > (0, 0, 0):
                    chosen.append((along_x, along_y, along_z))
    return chosen


def draw_rest_length(key, part):
    forward = forward_bonds()
    lengths = jnp.sqrt(jnp.array([float(vector[0] * vector[0] + vector[1] * vector[1] + vector[2] * vector[2]) for vector in forward], jnp.float32))
    spread = 0.04 * jnp.tanh(jax.random.normal(jax.random.fold_in(key, 21), (9, NX, NY, Z), jnp.float32))
    ahead = lengths[:, None, None, None] * (1.0 + spread)
    behind = [jnp.roll(ahead[position], (forward[position][0], forward[position][1], forward[position][2]), axis=(0, 1, 2)) for position in range(9)]
    lattice = jnp.concatenate([ahead, jnp.stack(behind)], axis=0).astype(jnp.float32)
    blocks = lattice.reshape(18, NX, YT, CY, ZT, CZ)
    ordered = jnp.transpose(blocks, (0, 1, 2, 4, 3, 5)).reshape(18, NX, YT * ZT, CY, CZ)
    return jnp.roll(ordered, -(ZT // 2), axis=2)


def draw_heights(key, part):
    values = jax.random.randint(jax.random.fold_in(key, 31), (NX * NY,), Z // 2, Z + 1)
    spots = jax.random.permutation(jax.random.fold_in(key, 32), NX * NY)
    values = values.at[spots[0]].set(Z).at[spots[1]].set(Z // 2)
    return values.reshape(NX, NY).astype(jnp.int32)


def levels(rng, dims, split, smallest, top_value):
    def one(axis_at, blocks):
        steps = jax.random.uniform(jax.random.fold_in(jax.random.fold_in(rng, 6), axis_at), (blocks,), jnp.float32, smallest / len(split), top_value / len(split))
        return jnp.repeat(jnp.exp(steps), dims[axis_at] // blocks).reshape((-1,) + (1,) * (len(dims) - axis_at - 1))

    factor_of = one(*split[0])
    for cut in split[1:]:
        factor_of = factor_of * one(*cut)
    return factor_of


def gaussian(own_key, shape, scale, limit, shards=(), dtype=jnp.bfloat16):
    level = levels(own_key, shape, shards, -0.22, 0.18) if shards else 1.0
    entries = jax.random.normal(own_key, shape, jnp.float32) * scale * level
    return jnp.minimum(jnp.maximum(entries, -limit), limit).astype(dtype)


def setup_inputs(seed: int = 0) -> dict:
    key_of = jax.random.split(jax.random.key(seed), 5)
    displacement = gaussian(key_of[0], (3, NX, TILES, CY, CZ), 0.016, 0.04, ((1, 2), (2, 16)), jnp.float32)
    velocity = gaussian(key_of[1], (3, NX, TILES, CY, CZ), 1.0, 5.0, ((1, 2), (2, 16)), jnp.float32)
    rest_length = draw_rest_length(jax.random.fold_in(key_of[4], 71), 0)
    heights = draw_heights(jax.random.fold_in(key_of[4], 71), 0)
    return dict(displacement=displacement, velocity=velocity, rest_length=rest_length, heights=heights)


CUTOFF = 1.5
REACH_RADIUS = 3.5
DENSITY_DECAY = 3.0
PAIR_DECAY = 6.0
PAIR_SCALE = 0.6
EMBED_SCALE = 1.0
DENSITY_FLOOR = 0.5
SHARPNESS = 8.0
STRAIN_LIMIT = 0.1
BIAS_SCALE = 0.08
KICK_FACTOR = 0.2
TIME_STEP = 0.05
THERMAL = 0.5

def list_offsets(reach_sq, forward_only):
    chosen = []
    for along_x in range(-3, 4):
        for along_y in range(-3, 4):
            for along_z in range(-3, 4):
                length_sq = along_x * along_x + along_y * along_y + along_z * along_z
                if 0 < length_sq <= reach_sq:
                    if not forward_only or (along_x, along_y, along_z) > (0, 0, 0):
                        chosen.append((along_x, along_y, along_z))
    return chosen

def bond_offsets():
    forward = list_offsets(2, True)
    return forward + [(-vector[0], -vector[1], -vector[2]) for vector in forward]

def taper_value(radius, cutoff):
    inside = 1.0 - (radius / cutoff) ** 2
    return jnp.where(radius < cutoff, inside * inside, 0.0)

def taper_slope(radius, cutoff):
    inside = 1.0 - (radius / cutoff) ** 2
    return jnp.where(radius < cutoff, -4.0 * radius * inside / (cutoff * cutoff), 0.0)

def to_lattice(tiled):
    channels, row_count = (tiled.shape[0], tiled.shape[1])
    ordered = jnp.roll(tiled, ZT // 2, axis=2)
    blocks = ordered.reshape(channels, row_count, YT, ZT, CY, CZ)
    return jnp.transpose(blocks, (0, 1, 2, 4, 3, 5)).reshape(channels, row_count, YT * CY, ZT * CZ)

def to_tiles(lattice):
    channels, row_count = (lattice.shape[0], lattice.shape[1])
    blocks = lattice.reshape(channels, row_count, YT, CY, ZT, CZ)
    ordered = jnp.transpose(blocks, (0, 1, 2, 4, 3, 5)).reshape(channels, row_count, YT * ZT, CY, CZ)
    return jnp.roll(ordered, -(ZT // 2), axis=2)

def shifted(source, offset):
    rolled = jnp.roll(source, (-offset[0], -offset[1]), axis=(-3, -2))
    padded = jnp.pad(rolled, [(0, 0)] * (source.ndim - 1) + [(3, 3)])
    layers = source.shape[-1]
    return padded[..., 3 + offset[2]:3 + offset[2] + layers]

def separation(displacement, offset):
    beside = shifted(displacement, offset)
    pieces = [offset[component] + beside[component] - displacement[component] for component in range(3)]
    radius = jnp.sqrt(pieces[0] * pieces[0] + pieces[1] * pieces[1] + pieces[2] * pieces[2])
    return (pieces, radius)

def reference(displacement, velocity, rest_length, heights):
    displacement = to_lattice(displacement)
    velocity = to_lattice(velocity)
    rest_length = to_lattice(rest_length)
    layers = displacement.shape[-1]
    layer_index = lax.broadcasted_iota(jnp.int32, (heights.shape[0], heights.shape[1], layers), 2)
    present = (layer_index < heights[:, :, None]).astype(jnp.float32)
    bond_list = bond_offsets()
    reach_list = list_offsets(9, False)
    density = jnp.zeros(present.shape, jnp.float32)
    bond_energy = jnp.zeros(present.shape, jnp.float32)
    bond_room = jnp.zeros(present.shape, jnp.float32)
    for bond_index in range(18):
        offset = bond_list[bond_index]
        pieces, radius = separation(displacement, offset)
        partner = shifted(present, offset)
        paired = present * partner
        density = density + partner * jnp.exp(-DENSITY_DECAY * (radius - 1.0)) * taper_value(radius, CUTOFF)
        relative = (radius - rest_length[bond_index]) / (rest_length[bond_index] * STRAIN_LIMIT)
        squared = relative * relative
        bond_energy = bond_energy + paired * jnp.exp(SHARPNESS * squared)
        bond_room = bond_room + paired * (1.0 - squared)
    embed_slope = -0.5 * EMBED_SCALE / jnp.sqrt(density + DENSITY_FLOOR)
    smooth_total = 1.0 + bond_energy
    for offset in reach_list:
        pieces, radius = separation(displacement, offset)
        smooth_total = smooth_total + taper_value(radius, REACH_RADIUS) * shifted(bond_energy, offset)
    smooth_max = jnp.log(smooth_total) / SHARPNESS
    bias_gain = BIAS_SCALE / (1.0 + smooth_max * smooth_max)
    bias_energy = present * bias_gain * bond_room
    adjoint_total = present * bond_room * BIAS_SCALE * (-2.0 * smooth_max) / (1.0 + smooth_max * smooth_max) ** 2 / (SHARPNESS * smooth_total)
    forces = [jnp.zeros(present.shape, jnp.float32) for component in range(3)]
    adjoint_lambda = adjoint_total
    for offset in reach_list:
        pieces, radius = separation(displacement, offset)
        far_adjoint = shifted(adjoint_total, offset)
        far_energy = shifted(bond_energy, offset)
        weight = (adjoint_total * far_energy + far_adjoint * bond_energy) * taper_slope(radius, REACH_RADIUS) / radius
        forces = [forces[component] + weight * pieces[component] for component in range(3)]
        adjoint_lambda = adjoint_lambda + taper_value(radius, REACH_RADIUS) * far_adjoint
    for bond_index in range(18):
        offset = bond_list[bond_index]
        pieces, radius = separation(displacement, offset)
        paired = present * shifted(present, offset)
        cut_value = taper_value(radius, CUTOFF)
        cut_slope = taper_slope(radius, CUTOFF)
        density_slope = jnp.exp(-DENSITY_DECAY * (radius - 1.0)) * (cut_slope - DENSITY_DECAY * cut_value)
        pair_slope = PAIR_SCALE * jnp.exp(-PAIR_DECAY * (radius - 1.0)) * (cut_slope - PAIR_DECAY * cut_value)
        relative = (radius - rest_length[bond_index]) / (rest_length[bond_index] * STRAIN_LIMIT)
        squared = relative * relative
        lifted = jnp.exp(SHARPNESS * squared)
        strain_slope = 2.0 * relative / (rest_length[bond_index] * STRAIN_LIMIT)
        far_slope = shifted(embed_slope, offset)
        far_gain = shifted(bias_gain, offset)
        far_lambda = shifted(adjoint_lambda, offset)
        coupled = paired * (pair_slope + (embed_slope + far_slope) * density_slope + (SHARPNESS * (adjoint_lambda + far_lambda) * lifted - bias_gain - far_gain) * strain_slope)
        weight = coupled / radius
        forces = [forces[component] + weight * pieces[component] for component in range(3)]
    half_velocity = velocity + KICK_FACTOR * jnp.stack(forces)
    new_displacement = displacement + TIME_STEP * half_velocity
    boost_factor = jnp.sum(present * jnp.exp(bias_energy / THERMAL)) / jnp.sum(present)
    return (to_tiles(new_displacement), to_tiles(half_velocity), boost_factor)
```

```python
import functools

import jax
import jax.numpy as jnp
from jax import lax
from jax.experimental import pallas as pl
from jax.experimental.pallas import tpu as pltpu
from jax.sharding import PartitionSpec as P

CUTOFF_SQ = 1.5 * 1.5
REACH_SQ = 3.5 * 3.5
F32 = jnp.float32
MESH = pl.DeviceIdType.MESH


def list_offsets(reach_sq, forward_only):
    chosen = []
    for ax in range(-3, 4):
        for ay in range(-3, 4):
            for az in range(-3, 4):
                length_sq = ax * ax + ay * ay + az * az
                if 0 < length_sq <= reach_sq:
                    if not forward_only or (ax, ay, az) > (0, 0, 0):
                        chosen.append((ax, ay, az))
    return chosen


FORWARD = list_offsets(2, True)
BONDS = FORWARD + [(-v[0], -v[1], -v[2]) for v in FORWARD]
REACH = list_offsets(9, False)
ROUNDS = [(3, 0, 3), (1, 3, 3), (1, 4, 3), (1, 5, 1), (2, 6, 1)]


def kernel(n_gx, n_yz, z_tiles, heights, disp, vel, rest, new_disp, new_vel, boost, *scratch):
    xr, yr, zr, ys, zs = (scratch[i:25:5] for i in range(5))
    (store, zb, hb, ins, bonds, part, first, sums, send_sem, recv_sem, red_send, red_recv) = scratch[25:]
    nx_all, ny_all = heights.shape
    planes, rows, cols = disp.shape[1], disp.shape[3], disp.shape[4]
    y_tiles = n_yz // z_tiles
    gx = lax.axis_index("gx")
    me = lax.axis_index("yz")
    h = me + z_tiles // 2
    y_tile = lax.rem(h // z_tiles, y_tiles)
    z_tile = lax.rem(h, z_tiles)
    x_steps = [0, 1] if n_gx == 2 else [0, 1, -1]
    n_slots = len(x_steps)
    steps = [0, 1, -1]

    def target(a, b, c):
        to_y = lax.rem(y_tile + b + y_tiles, y_tiles)
        to_z = lax.rem(z_tile + c + z_tiles, z_tiles)
        to = lax.rem(to_y * z_tiles + to_z + n_yz - z_tiles // 2, n_yz)
        return (lax.rem(gx + a + n_gx, n_gx), to)

    n_dev = n_gx * n_yz
    rank = gx * n_yz + me
    barrier = pltpu.get_barrier_semaphore()

    def greet(k, carry):
        to = lax.rem(rank + k, n_dev)
        pl.semaphore_signal(barrier, inc=1, device_id=(to // n_yz, lax.rem(to, n_yz)), device_id_type=MESH)
        return carry

    lax.fori_loop(1, n_dev, greet, 0)

    lane = lax.broadcasted_iota(jnp.int32, (8, 128), 1)

    def messages(r):
        out = []
        for ai, a in enumerate(x_steps):
            if ai:
                out.append((xr[r].at[0], xr[r].at[ai], a, 0, 0))
        for bi in range(2):
            for ai, a in enumerate(x_steps):
                out.append((ys[r].at[bi], yr[r].at[bi, ai], a, steps[1 + bi], 0))
        for ci in range(2):
            for bi, b in enumerate(steps):
                for ai, a in enumerate(x_steps):
                    out.append((zs[r].at[ci], zr[r].at[ci, bi, ai], a, b, steps[1 + ci]))
        return [
            pltpu.make_async_remote_copy(
                src_ref=src,
                dst_ref=dst,
                send_sem=send_sem.at[r, i],
                recv_sem=recv_sem.at[r, i],
                device_id=target(a, b, c),
                device_id_type=MESH,
            )
            for i, (src, dst, a, b, c) in enumerate(out)
        ]

    def pack(r):
        count = ROUNDS[r][0]
        up = jnp.zeros((8, 128), F32)
        down = jnp.zeros((8, 128), F32)
        for q in range(count):
            for p in range(planes):
                item = q * planes + p
                low = xr[r][0, q, p, :, 0:128]
                high = xr[r][0, q, p, :, cols - 128 : cols]
                here = (lane >= 4 * item) & (lane < 4 * item + 4)
                up = jnp.where(here, pltpu.roll(high, (4 * item + 4) % 128, 1), up)
                down = jnp.where(here, pltpu.roll(low, (4 * item) % 128, 1), down)
                ys[r][0, q, p] = xr[r][0, q, p, rows - 4 : rows, :]
                ys[r][1, q, p] = xr[r][0, q, p, 0:4, :]
        zs[r][0] = up
        zs[r][1] = down

    def send(r):
        pack(r)
        for copy in messages(r):
            copy.start()

    def receive(r):
        for copy in messages(r):
            copy.wait_recv()
        count, base, halo = ROUNDS[r]
        for ai in range(n_slots):
            for ci in range(2):
                inside = z_tile > 0 if ci == 0 else z_tile < z_tiles - 1
                keep = jnp.where(inside, 1.0, 0.0).astype(F32)
                zb[ai, ci, 4:12] = zr[r][ci, 0, ai] * keep
                zb[ai, ci, 0:4] = zr[r][ci, 1, ai, 4:8] * keep
                zb[ai, ci, 12:16] = zr[r][ci, 2, ai, 0:4] * keep

        def one(xp, carry):
            plane = lax.rem(xp + 1, planes)
            group = (xp + 1) // planes
            slot = lax.rem(group + 1, 2) if n_gx == 2 else lax.rem(4 - group, 3)
            for q in range(count):
                for half in range(2):
                    span = slice(half * 128, half * 128 + 128)
                    store[base + q, 3, half, xp, 4:12] = xr[r][slot, q, plane, :, span]
                    store[base + q, 3, half, xp, 0:4] = yr[r][0, slot, q, plane, :, span]
                    store[base + q, 3, half, xp, 12:16] = yr[r][1, slot, q, plane, :, span]
            for q in range(count):
                item = q * planes + plane
                for rt in range(2):
                    band = slice(8 * rt, 8 * rt + 8)
                    t1 = store[base + q, 3, 0, xp, band]
                    t2 = store[base + q, 3, 1, xp, band]
                    below = zb[slot, 0, band]
                    above = zb[slot, 1, band]
                    for dz in range(1, halo + 1):
                        r0 = pltpu.roll(below, lax.rem(124 + 128 - 4 * item + dz, 128), 1)
                        r1 = pltpu.roll(t1, dz, 1)
                        r2 = pltpu.roll(t2, dz, 1)
                        store[base + q, 3 - dz, 0, xp, band] = jnp.where(lane < dz, r0, r1)
                        store[base + q, 3 - dz, 1, xp, band] = jnp.where(lane < dz, r1, r2)
                        s1 = pltpu.roll(t1, 128 - dz, 1)
                        s2 = pltpu.roll(t2, 128 - dz, 1)
                        s3 = pltpu.roll(above, lax.rem(256 - 4 * item - dz, 128), 1)
                        store[base + q, 3 + dz, 0, xp, band] = jnp.where(lane >= 128 - dz, s2, s1)
                        store[base + q, 3 + dz, 1, xp, band] = jnp.where(lane >= 128 - dz, s3, s2)
            return carry

        lax.fori_loop(3 - halo, 3 + planes + halo, one, 0)

    def far(q, x, half, d):
        return store[q, d[2] + 3, half, x + 3 + d[0], 4 + d[1] : 12 + d[1]]

    def separation(x, half, d, mine):
        pieces = []
        for c in range(3):
            delta = far(c, x, half, d) - mine[c]
            pieces.append(delta + float(d[c]) if d[c] else delta)
        return pieces

    def own(q, x, half):
        return far(q, x, half, (0, 0, 0))

    def put(ref, q, x, half, value):
        @pl.when(half == 0)
        def _():
            ref[0, q, x, :, 0:128] = value

        @pl.when(half == 1)
        def _():
            ref[0, q, x, :, 128:256] = value

    def tiles(body):
        def step(i, carry):
            body(i, i // 2, lax.rem(i, 2))
            return carry

        lax.fori_loop(0, 2 * planes, step, 0)

    for q in range(3):
        for p in range(planes):
            xr[0][0, q, p] = disp[q, p, 0]

    def height_row(xp, carry):
        at_x = lax.rem(gx * planes + xp - 3 + nx_all, nx_all)
        for row in range(3, 13):
            at_y = lax.rem(y_tile * rows + row - 4 + ny_all, ny_all)
            hb[xp, row : row + 1] = jnp.full((1, 128), heights[at_x, at_y], jnp.int32)
        return carry

    lax.fori_loop(2, 4 + planes, height_row, 0)
    pl.semaphore_wait(barrier, n_dev - 1)
    send(0)
    receive(0)

    def bond_pass(i, x, half):
        mine = [own(c, x, half) for c in range(3)]
        layer = lane + (z_tile * cols + half * 128)
        here = layer < hb[x + 3, 4:12]
        density = jnp.zeros((8, 128), F32)
        energy = jnp.zeros((8, 128), F32)
        room = jnp.zeros((8, 128), F32)
        for k, d in enumerate(BONDS):
            s = separation(x, half, d, mine)
            r_sq = s[0] * s[0] + s[1] * s[1] + s[2] * s[2]
            inv_r = lax.rsqrt(r_sq)
            radius = r_sq * inv_r
            partner = layer + d[2] < hb[x + 3 + d[0], 4 + d[1] : 12 + d[1]]
            if d[2] < 0:
                partner = partner & (layer >= -d[2])
            paired = partner & here
            decay = jnp.exp(3.0 - 3.0 * radius)
            cut = jnp.maximum(1.0 - r_sq * (1.0 / CUTOFF_SQ), 0.0)
            cut_value = cut * cut
            length = rest_half(k, x, half)
            gain = 10.0 / length
            strain = (radius - length) * gain
            squared = strain * strain
            lifted = jnp.exp(8.0 * squared)
            density = density + jnp.where(partner, decay * cut_value, 0.0)
            energy = energy + jnp.where(paired, lifted, 0.0)
            room = room + jnp.where(paired, 1.0 - squared, 0.0)
            scale = jnp.where(paired, inv_r, 0.0)
            cut_slope = (-4.0 / CUTOFF_SQ) * radius * cut
            bonds[i, k, 0] = scale * 0.6 * (decay * decay) * (cut_slope - 6.0 * cut_value)
            bonds[i, k, 1] = scale * decay * (cut_slope - 3.0 * cut_value)
            strain_slope = scale * (2.0 * strain * gain)
            bonds[i, k, 2] = strain_slope * (8.0 * lifted)
            bonds[i, k, 3] = strain_slope
        put(xr[1], 0, x, half, energy)
        put(xr[4], 0, x, half, -0.5 * lax.rsqrt(density + 0.5))
        part[i, 0] = room

    def rest_half(k, x, half):
        return rest[k, x, 0, :, pl.ds(pl.multiple_of(half * 128, 128), 128)]

    tiles(bond_pass)
    send(1)

    def reach_pass(i, x, half):
        mine = [own(c, x, half) for c in range(3)]
        for k, d in enumerate(REACH):
            s = separation(x, half, d, mine)
            r_sq = s[0] * s[0] + s[1] * s[1] + s[2] * s[2]
            ins[i, k] = jnp.maximum(1.0 - r_sq * (1.0 / REACH_SQ), 0.0)

    tiles(reach_pass)
    receive(1)
    first[...] = jnp.zeros_like(first)

    def smooth_pass(i, x, half):
        energy = own(3, x, half)
        total = 1.0 + energy
        for k, d in enumerate(REACH):
            inside = ins[i, k]
            total = total + (inside * inside) * far(3, x, half, d)
        room = part[i, 0]
        smooth = jnp.log(total) * 0.125
        share = 1.0 / (1.0 + smooth * smooth)
        gain = 0.08 * share
        layer = lane + (z_tile * cols + half * 128)
        here = layer < hb[x + 3, 4:12]
        adjoint = room * 0.08 * (-2.0 * smooth) * (share * share) / (8.0 * total)
        put(xr[2], 0, x, half, jnp.where(here, adjoint, 0.0))
        put(xr[4], 1, x, half, gain)
        first[...] += jnp.where(here, jnp.exp(gain * room * 2.0), 0.0)

    tiles(smooth_pass)
    send(2)
    send(4)
    sums[0] = jnp.sum(first[...], axis=0, keepdims=True)

    def reduction(k):
        to = lax.rem(rank + k, n_dev)
        return pltpu.make_async_remote_copy(
            src_ref=sums.at[0],
            dst_ref=sums.at[k],
            send_sem=red_send.at[k],
            recv_sem=red_recv.at[k],
            device_id=(to // n_yz, lax.rem(to, n_yz)),
            device_id_type=MESH,
        )

    def spread(k, carry):
        reduction(k).start()
        return carry

    lax.fori_loop(1, n_dev, spread, 0)

    def pull(source):
        def run(i, x, half):
            mine = [own(c, x, half) for c in range(3)]
            total = [jnp.zeros((8, 128), F32) for _ in range(3)]
            for k, d in enumerate(REACH):
                s = separation(x, half, d, mine)
                weight = ins[i, k] * far(source, x, half, d)
                total = [total[c] + weight * s[c] for c in range(3)]
            return total

        return run

    def energy_pull(i, x, half):
        total = pull(3)(i, x, half)
        for c in range(3):
            part[i, 1 + c] = total[c]

    tiles(energy_pull)
    receive(2)

    def lambda_pass(i, x, half):
        total = own(4, x, half)
        for k, d in enumerate(REACH):
            inside = ins[i, k]
            total = total + (inside * inside) * far(4, x, half, d)
        put(xr[3], 0, x, half, total)

    tiles(lambda_pass)
    send(3)

    def adjoint_pull(i, x, half):
        total = pull(4)(i, x, half)
        adjoint = own(4, x, half)
        energy = own(3, x, half)
        for c in range(3):
            part[i, 1 + c] = (-4.0 / REACH_SQ) * (adjoint * part[i, 1 + c] + energy * total[c])

    tiles(adjoint_pull)
    receive(4)
    receive(3)

    def final_pass(i, x, half):
        mine = [own(c, x, half) for c in range(3)]
        lam, embed, gain = own(5, x, half), own(6, x, half), own(7, x, half)
        force = [part[i, 1 + c] for c in range(3)]
        for k, d in enumerate(BONDS):
            s = separation(x, half, d, mine)
            weight = (
                bonds[i, k, 0]
                + (embed + far(6, x, half, d)) * bonds[i, k, 1]
                + (lam + far(5, x, half, d)) * bonds[i, k, 2]
                - (gain + far(7, x, half, d)) * bonds[i, k, 3]
            )
            force = [force[c] + weight * s[c] for c in range(3)]
        span = pl.ds(pl.multiple_of(half * 128, 128), 128)
        for c in range(3):
            speed = vel[c, x, 0, :, span] + 0.2 * force[c]
            new_vel[c, x, 0, :, span] = speed
            new_disp[c, x, 0, :, span] = mine[c] + 0.05 * speed

    tiles(final_pass)

    def collect(k, carry):
        reduction(k).wait_recv()
        return carry

    lax.fori_loop(1, n_dev, collect, 0)
    atoms = jnp.zeros((), jnp.int32)

    def count_row(i, carry):
        return carry + jnp.clip(heights[i // ny_all, lax.rem(i, ny_all)], 0, z_tiles * cols)

    atoms = lax.fori_loop(0, nx_all * ny_all, count_row, atoms)
    total = jnp.sum(jnp.sum(sums[...], axis=0), axis=1, keepdims=True)
    boost[...] = jnp.broadcast_to(total, (1, 128)) / jnp.full((1, 128), atoms.astype(F32))

    def finish(k, carry):
        reduction(k).wait_send()
        return carry

    lax.fori_loop(1, n_dev, finish, 0)
    for r in range(5):
        for copy in messages(r):
            copy.wait_send()


def body(n_gx, n_yz, displacement, velocity, rest_length, heights):
    _, planes, _, rows, cols = displacement.shape
    z_tiles = n_yz // (heights.shape[1] // rows)
    slots = 2 if n_gx == 2 else 3
    n_dev = n_gx * n_yz
    n_msg = (slots - 1) + 2 * slots + 6 * slots
    scratch = []
    for count, _, _ in ROUNDS:
        scratch += [
            pltpu.VMEM((slots, count, planes, rows, cols), F32),
            pltpu.VMEM((2, slots, count, planes, 4, cols), F32),
            pltpu.VMEM((2, 3, slots, 8, 128), F32),
            pltpu.VMEM((2, count, planes, 4, cols), F32),
            pltpu.VMEM((2, 8, 128), F32),
        ]
    scratch += [
        pltpu.VMEM((8, 7, 2, planes + 6, 16, 128), F32),
        pltpu.VMEM((slots, 2, 16, 128), F32),
        pltpu.VMEM((planes + 6, 16, 128), jnp.int32),
        pltpu.VMEM((2 * planes, len(REACH), 8, 128), F32),
        pltpu.VMEM((2 * planes, len(BONDS), 4, 8, 128), F32),
        pltpu.VMEM((2 * planes, 4, 8, 128), F32),
        pltpu.VMEM((8, 128), F32),
        pltpu.VMEM((n_dev, 1, 128), F32),
        pltpu.SemaphoreType.DMA((len(ROUNDS), n_msg)),
        pltpu.SemaphoreType.DMA((len(ROUNDS), n_msg)),
        pltpu.SemaphoreType.DMA((n_dev,)),
        pltpu.SemaphoreType.DMA((n_dev,)),
    ]
    vmem = pl.BlockSpec(memory_space=pltpu.VMEM)
    new_disp, new_vel, boost = pl.pallas_call(
        functools.partial(kernel, n_gx, n_yz, z_tiles),
        out_shape=(
            jax.ShapeDtypeStruct(displacement.shape, F32),
            jax.ShapeDtypeStruct(velocity.shape, F32),
            jax.ShapeDtypeStruct((1, 128), F32),
        ),
        in_specs=[pl.BlockSpec(memory_space=pltpu.SMEM), vmem, vmem, vmem],
        out_specs=(vmem, vmem, vmem),
        scratch_shapes=scratch,
        compiler_params=pltpu.CompilerParams(
            collective_id=0, has_side_effects=True, vmem_limit_bytes=48 * 1024 * 1024
        ),
    )(heights, displacement, velocity, rest_length)
    return new_disp, new_vel, boost[0, 0]


def solution(mesh):
    tiled = P(None, "gx", "yz", None, None)
    sizes = (mesh.shape["gx"], mesh.shape["yz"])
    return jax.shard_map(
        functools.partial(body, *sizes),
        mesh=mesh,
        in_specs=(tiled, tiled, tiled, P()),
        out_specs=(tiled, tiled, P()),
        check_vma=False,
    )
```

```python
import functools

import jax
import jax.numpy as jnp
from jax import lax
from jax.experimental import pallas as pl
from jax.experimental.pallas import tpu as pltpu
from jax.sharding import PartitionSpec as P

CUTOFF_SQ = 1.5 * 1.5
REACH_SQ = 3.5 * 3.5
F32 = jnp.float32
MESH = pl.DeviceIdType.MESH


def list_offsets(reach_sq, forward_only):
    chosen = []
    for ax in range(-3, 4):
        for ay in range(-3, 4):
            for az in range(-3, 4):
                length_sq = ax * ax + ay * ay + az * az
                if 0 < length_sq <= reach_sq:
                    if not forward_only or (ax, ay, az) > (0, 0, 0):
                        chosen.append((ax, ay, az))
    return chosen


FORWARD = list_offsets(2, True)
BONDS = FORWARD + [(-v[0], -v[1], -v[2]) for v in FORWARD]
REACH = list_offsets(9, False)
ROUNDS = [(3, 0, 3), (1, 3, 3), (1, 4, 3), (1, 5, 1), (2, 6, 1)]


def kernel(n_gx, n_yz, z_tiles, heights_hbm, disp, rest_hbm, forces, boost, *scratch):
    xr, yr, zr, ys, zs = (scratch[i:25:5] for i in range(5))
    (store, zb, hb, ins, bonds, part, first, sums, send_sem, recv_sem, red_send, red_recv, rest, heights, load_sem) = scratch[25:]
    nx_all, ny_all = heights.shape
    loads = [
        pltpu.make_async_copy(heights_hbm, heights, load_sem.at[0]),
        pltpu.make_async_copy(disp.at[:, :, 0], xr[0].at[0], load_sem.at[1]),
        pltpu.make_async_copy(rest_hbm, rest, load_sem.at[2]),
    ]
    for load in loads:
        load.start()
    planes, rows, cols = disp.shape[1], disp.shape[3], disp.shape[4]
    y_tiles = n_yz // z_tiles
    gx = lax.axis_index("gx")
    me = lax.axis_index("yz")
    h = me + z_tiles // 2
    y_tile = lax.rem(h // z_tiles, y_tiles)
    z_tile = lax.rem(h, z_tiles)
    x_steps = [0, 1] if n_gx == 2 else [0, 1, -1]
    n_slots = len(x_steps)
    steps = [0, 1, -1]

    def target(a, b, c):
        to_y = lax.rem(y_tile + b + y_tiles, y_tiles)
        to_z = lax.rem(z_tile + c + z_tiles, z_tiles)
        to = lax.rem(to_y * z_tiles + to_z + n_yz - z_tiles // 2, n_yz)
        return (lax.rem(gx + a + n_gx, n_gx), to)

    n_dev = n_gx * n_yz
    rank = gx * n_yz + me
    barrier = pltpu.get_barrier_semaphore()

    def greet(k, carry):
        to = lax.rem(rank + k, n_dev)
        pl.semaphore_signal(barrier, inc=1, device_id=(to // n_yz, lax.rem(to, n_yz)), device_id_type=MESH)
        return carry

    lax.fori_loop(1, n_dev, greet, 0)

    lane = lax.broadcasted_iota(jnp.int32, (8, 128), 1)

    left_slot = 1
    right_slot = n_slots - 1
    last_tile = z_tile == z_tiles - 1
    first_tile = z_tile == 0

    def messages(r):
        halo = ROUNDS[r][2]
        out = []
        if halo == 1:
            edge = planes - 1
            out.append((xr[r].at[0, :, edge], xr[r].at[left_slot, :, edge], 1, 0, 0))
            out.append((xr[r].at[0, :, 0], xr[r].at[right_slot, :, 0], -1, 0, 0))
        else:
            for ai in range(1, n_slots):
                out.append((xr[r].at[0], xr[r].at[ai], x_steps[ai], 0, 0))
        for ai, a in reversed(list(enumerate(x_steps))):
            for bi in range(2):
                out.append((ys[r].at[bi], yr[r].at[bi, ai], a, steps[1 + bi], 0))
        for ci in range(2):
            for ai, a in enumerate(x_steps):
                for bi in range(2):
                    out.append((zs[r].at[ci, 1 - bi], zr[r].at[ci, ai, 2 + bi], a, steps[1 + bi], steps[1 + ci]))
                out.append((zs[r].at[ci], zr[r].at[ci, ai, 0:2], a, 0, steps[1 + ci]))
        return [
            (
                c,
                pltpu.make_async_remote_copy(
                    src_ref=src,
                    dst_ref=dst,
                    send_sem=send_sem.at[r, i],
                    recv_sem=recv_sem.at[r, i],
                    device_id=target(a, b, c),
                    device_id_type=MESH,
                ),
            )
            for i, (src, dst, a, b, c) in enumerate(out)
        ]

    def along(r, step, act, sending):
        chosen = [copy for c, copy in messages(r) if c == step]
        edge = last_tile if (step > 0) == sending else first_tile
        if step == 0:
            for copy in chosen:
                act(copy)
        else:

            @pl.when(jnp.logical_not(edge))
            def _():
                for copy in chosen:
                    act(copy)

    def pack(r):
        count, _, halo = ROUNDS[r]
        up = jnp.zeros((8, 128), F32)
        down = jnp.zeros((8, 128), F32)
        for q in range(count):
            for p in range(planes):
                item = q * planes + p
                low = xr[r][0, q, p, :, 0:128]
                high = xr[r][0, q, p, :, cols - 128 : cols]
                here = (lane >= 4 * item) & (lane < 4 * item + 4)
                up = jnp.where(here, pltpu.roll(high, (4 * item + 4) % 128, 1), up)
                down = jnp.where(here, pltpu.roll(low, (4 * item) % 128, 1), down)
                for half in range(2):
                    at = ((q * 2 + half) * planes + p) * halo
                    span = slice(half * 128, half * 128 + 128)
                    ys[r][0, at : at + halo] = xr[r][0, q, p, rows - halo : rows, span]
                    ys[r][1, at : at + halo] = xr[r][0, q, p, 0:halo, span]
        zs[r][0, 0], zs[r][0, 1] = up[0:4], up[4:8]
        zs[r][1, 0], zs[r][1, 1] = down[0:4], down[4:8]

    def send(r):
        if r:
            pack(r)
        for step in steps:
            along(r, step, lambda copy: copy.start(), True)

    def receive(r):
        for step in steps:
            along(r, step, lambda copy: copy.wait_recv(), False)
        count, base, halo = ROUNDS[r]
        for ci in range(2):
            edge = first_tile if ci == 0 else last_tile

            @pl.when(edge)
            def _():
                for ai in range(n_slots):
                    zb[ai, ci] = jnp.zeros((16, 128), F32)

            @pl.when(jnp.logical_not(edge))
            def _():
                for ai in range(n_slots):
                    zb[ai, ci, 0:4] = zr[r][ci, ai, 2]
                    zb[ai, ci, 4:8] = zr[r][ci, ai, 0]
                    zb[ai, ci, 8:12] = zr[r][ci, ai, 1]
                    zb[ai, ci, 12:16] = zr[r][ci, ai, 3]

        def one(xp, carry):
            plane = lax.rem(xp + 1, planes)
            group = (xp + 1) // planes
            slot = lax.rem(group + 1, 2) if n_gx == 2 else lax.rem(4 - group, 3)
            for q in range(count):
                for half in range(2):
                    span = slice(half * 128, half * 128 + 128)
                    store[base + q, 3, half, xp, 4:12] = xr[r][slot, q, plane, :, span]
                    at = ((q * 2 + half) * planes + plane) * halo
                    store[base + q, 3, half, xp, 4 - halo : 4] = yr[r][0, slot, pl.ds(at, halo)]
                    store[base + q, 3, half, xp, 12 : 12 + halo] = yr[r][1, slot, pl.ds(at, halo)]
            for q in range(count):
                item = q * planes + plane
                for rt in range(2):
                    band = slice(8 * rt, 8 * rt + 8)
                    t1 = store[base + q, 3, 0, xp, band]
                    t2 = store[base + q, 3, 1, xp, band]
                    below = zb[slot, 0, band]
                    above = zb[slot, 1, band]
                    for dz in range(1, halo + 1):
                        r0 = pltpu.roll(below, lax.rem(124 + 128 - 4 * item + dz, 128), 1)
                        r1 = pltpu.roll(t1, dz, 1)
                        r2 = pltpu.roll(t2, dz, 1)
                        store[base + q, 3 - dz, 0, xp, band] = jnp.where(lane < dz, r0, r1)
                        store[base + q, 3 - dz, 1, xp, band] = jnp.where(lane < dz, r1, r2)
                        s1 = pltpu.roll(t1, 128 - dz, 1)
                        s2 = pltpu.roll(t2, 128 - dz, 1)
                        s3 = pltpu.roll(above, lax.rem(256 - 4 * item - dz, 128), 1)
                        store[base + q, 3 + dz, 0, xp, band] = jnp.where(lane >= 128 - dz, s2, s1)
                        store[base + q, 3 + dz, 1, xp, band] = jnp.where(lane >= 128 - dz, s3, s2)
            return carry

        lax.fori_loop(3 - halo, 3 + planes + halo, one, 0)

    def far(q, x, half, d):
        return store[q, d[2] + 3, half, x + 3 + d[0], 4 + d[1] : 12 + d[1]]

    def separation(x, half, d, mine):
        pieces = []
        for c in range(3):
            delta = far(c, x, half, d) - mine[c]
            pieces.append(delta + float(d[c]) if d[c] else delta)
        return pieces

    def own(q, x, half):
        return far(q, x, half, (0, 0, 0))

    def put(ref, q, x, half, value):
        @pl.when(half == 0)
        def _():
            ref[0, q, x, :, 0:128] = value

        @pl.when(half == 1)
        def _():
            ref[0, q, x, :, 128:256] = value

    def tiles(body):
        def step(i, carry):
            body(i, i // 2, lax.rem(i, 2))
            return carry

        lax.fori_loop(0, 2 * planes, step, 0)

    loads[0].wait()

    def height_row(xp, carry):
        at_x = lax.rem(gx * planes + xp - 3 + nx_all, nx_all)
        for row in range(3, 13):
            at_y = lax.rem(y_tile * rows + row - 4 + ny_all, ny_all)
            hb[xp, row : row + 1] = jnp.full((1, 128), heights[at_x, at_y], jnp.int32)
        return carry

    lax.fori_loop(2, 4 + planes, height_row, 0)
    loads[1].wait()
    pack(0)
    pl.semaphore_wait(barrier, n_dev - 1)
    send(0)

    def count_column(i, carry):
        for j in range(ny_all):
            carry = carry + jnp.clip(heights[i, j], 0, z_tiles * cols)
        return carry

    atoms = lax.fori_loop(0, nx_all, count_column, jnp.zeros((), jnp.int32))
    loads[2].wait()
    receive(0)

    def bond_pass(i, x, half):
        mine = [own(c, x, half) for c in range(3)]
        layer = lane + (z_tile * cols + half * 128)
        here = layer < hb[x + 3, 4:12]
        density = jnp.zeros((8, 128), F32)
        energy = jnp.zeros((8, 128), F32)
        room = jnp.zeros((8, 128), F32)
        for k, d in enumerate(BONDS):
            s = separation(x, half, d, mine)
            r_sq = s[0] * s[0] + s[1] * s[1] + s[2] * s[2]
            inv_r = lax.rsqrt(r_sq)
            radius = r_sq * inv_r
            partner = layer + d[2] < hb[x + 3 + d[0], 4 + d[1] : 12 + d[1]]
            if d[2] < 0:
                partner = partner & (layer >= -d[2])
            paired = partner & here
            decay = jnp.exp(3.0 - 3.0 * radius)
            cut = jnp.maximum(1.0 - r_sq * (1.0 / CUTOFF_SQ), 0.0)
            cut_value = cut * cut
            length = rest_half(k, x, half)
            gain = 10.0 / length
            strain = (radius - length) * gain
            squared = strain * strain
            lifted = jnp.exp(8.0 * squared)
            density = density + jnp.where(partner, decay * cut_value, 0.0)
            energy = energy + jnp.where(paired, lifted, 0.0)
            room = room + jnp.where(paired, 1.0 - squared, 0.0)
            scale = jnp.where(paired, inv_r, 0.0)
            cut_slope = (-4.0 / CUTOFF_SQ) * radius * cut
            bonds[i, k, 0] = scale * 0.6 * (decay * decay) * (cut_slope - 6.0 * cut_value)
            bonds[i, k, 1] = scale * decay * (cut_slope - 3.0 * cut_value)
            strain_slope = scale * (2.0 * strain * gain)
            bonds[i, k, 2] = strain_slope * (8.0 * lifted)
            bonds[i, k, 3] = strain_slope
        put(xr[1], 0, x, half, energy)
        put(xr[4], 0, x, half, -0.5 * lax.rsqrt(density + 0.5))
        part[i, 0] = room

    def rest_half(k, x, half):
        return rest[k, x, 0, :, pl.ds(pl.multiple_of(half * 128, 128), 128)]

    tiles(bond_pass)
    send(1)

    def reach_pass(i, x, half):
        mine = [own(c, x, half) for c in range(3)]
        for k, d in enumerate(REACH):
            s = separation(x, half, d, mine)
            r_sq = s[0] * s[0] + s[1] * s[1] + s[2] * s[2]
            ins[i, k] = jnp.maximum(1.0 - r_sq * (1.0 / REACH_SQ), 0.0)

    tiles(reach_pass)
    receive(1)
    first[...] = jnp.zeros_like(first)

    def smooth_pass(i, x, half):
        energy = own(3, x, half)
        total = 1.0 + energy
        for k, d in enumerate(REACH):
            inside = ins[i, k]
            total = total + (inside * inside) * far(3, x, half, d)
        room = part[i, 0]
        smooth = jnp.log(total) * 0.125
        share = 1.0 / (1.0 + smooth * smooth)
        gain = 0.08 * share
        layer = lane + (z_tile * cols + half * 128)
        here = layer < hb[x + 3, 4:12]
        adjoint = room * 0.08 * (-2.0 * smooth) * (share * share) / (8.0 * total)
        put(xr[2], 0, x, half, jnp.where(here, adjoint, 0.0))
        put(xr[4], 1, x, half, gain)
        first[...] += jnp.where(here, jnp.exp(gain * room * 2.0), 0.0)

    tiles(smooth_pass)
    send(2)
    send(4)
    sums[0] = jnp.sum(first[...], axis=0, keepdims=True)

    def reduction(k):
        to = lax.rem(rank + k, n_dev)
        return pltpu.make_async_remote_copy(
            src_ref=sums.at[0],
            dst_ref=sums.at[k],
            send_sem=red_send.at[k],
            recv_sem=red_recv.at[k],
            device_id=(to // n_yz, lax.rem(to, n_yz)),
            device_id_type=MESH,
        )

    def spread(k, carry):
        reduction(k).start()
        return carry

    lax.fori_loop(1, n_dev, spread, 0)

    def pull(source):
        def run(i, x, half):
            mine = [own(c, x, half) for c in range(3)]
            total = [jnp.zeros((8, 128), F32) for _ in range(3)]
            for k, d in enumerate(REACH):
                s = separation(x, half, d, mine)
                weight = ins[i, k] * far(source, x, half, d)
                total = [total[c] + weight * s[c] for c in range(3)]
            return total

        return run

    def energy_pull(i, x, half):
        total = pull(3)(i, x, half)
        for c in range(3):
            part[i, 1 + c] = total[c]

    tiles(energy_pull)
    receive(2)

    def lambda_pass(i, x, half):
        total = own(4, x, half)
        for k, d in enumerate(REACH):
            inside = ins[i, k]
            total = total + (inside * inside) * far(4, x, half, d)
        put(xr[3], 0, x, half, total)

    tiles(lambda_pass)
    send(3)

    def adjoint_pull(i, x, half):
        total = pull(4)(i, x, half)
        adjoint = own(4, x, half)
        energy = own(3, x, half)
        for c in range(3):
            part[i, 1 + c] = (-4.0 / REACH_SQ) * (adjoint * part[i, 1 + c] + energy * total[c])

    tiles(adjoint_pull)
    receive(4)

    def final_pass(i, x, half):
        mine = [own(c, x, half) for c in range(3)]
        lam, embed, gain = own(5, x, half), own(6, x, half), own(7, x, half)
        force = [part[i, 1 + c] for c in range(3)]
        for k, d in enumerate(BONDS):
            s = separation(x, half, d, mine)
            weight = (
                bonds[i, k, 0]
                + (embed + far(6, x, half, d)) * bonds[i, k, 1]
                + (lam + far(5, x, half, d)) * bonds[i, k, 2]
                - (gain + far(7, x, half, d)) * bonds[i, k, 3]
            )
            force = [force[c] + weight * s[c] for c in range(3)]
        span = pl.ds(pl.multiple_of(half * 128, 128), 128)
        for c in range(3):
            forces[c, x, 0, :, span] = force[c]

    def collect(k, carry):
        reduction(k).wait_recv()
        return carry

    lax.fori_loop(1, n_dev, collect, 0)
    total = jnp.sum(jnp.sum(sums[...], axis=0), axis=1, keepdims=True)
    boost[...] = jnp.broadcast_to(total, (1, 128)) / jnp.full((1, 128), atoms.astype(F32))

    receive(3)
    tiles(final_pass)

    def finish(k, carry):
        reduction(k).wait_send()
        return carry

    lax.fori_loop(1, n_dev, finish, 0)
    for r in range(5):
        for step in steps:
            along(r, step, lambda copy: copy.wait_send(), True)


def body(n_gx, n_yz, displacement, velocity, rest_length, heights):
    _, planes, _, rows, cols = displacement.shape
    z_tiles = n_yz // (heights.shape[1] // rows)
    slots = 2 if n_gx == 2 else 3
    n_dev = n_gx * n_yz
    n_msg = 2 + 2 * slots + 6 * slots
    scratch = []
    for count, _, halo in ROUNDS:
        y_rows = count * 2 * planes * halo
        scratch += [
            pltpu.VMEM((slots, count, planes, rows, cols), F32),
            pltpu.VMEM((2, slots, y_rows, 128), F32),
            pltpu.VMEM((2, slots, 4, 4, 128), F32),
            pltpu.VMEM((2, y_rows, 128), F32),
            pltpu.VMEM((2, 2, 4, 128), F32),
        ]
    scratch += [
        pltpu.VMEM((8, 7, 2, planes + 6, 16, 128), F32),
        pltpu.VMEM((slots, 2, 16, 128), F32),
        pltpu.VMEM((planes + 6, 16, 128), jnp.int32),
        pltpu.VMEM((2 * planes, len(REACH), 8, 128), F32),
        pltpu.VMEM((2 * planes, len(BONDS), 4, 8, 128), F32),
        pltpu.VMEM((2 * planes, 4, 8, 128), F32),
        pltpu.VMEM((8, 128), F32),
        pltpu.VMEM((n_dev, 1, 128), F32),
        pltpu.SemaphoreType.DMA((len(ROUNDS), n_msg)),
        pltpu.SemaphoreType.DMA((len(ROUNDS), n_msg)),
        pltpu.SemaphoreType.DMA((n_dev,)),
        pltpu.SemaphoreType.DMA((n_dev,)),
        pltpu.VMEM(rest_length.shape, F32),
        pltpu.SMEM(heights.shape, jnp.int32),
        pltpu.SemaphoreType.DMA((3,)),
    ]
    vmem = pl.BlockSpec(memory_space=pltpu.VMEM)
    hbm = pl.BlockSpec(memory_space=pltpu.HBM)
    forces, boost = pl.pallas_call(
        functools.partial(kernel, n_gx, n_yz, z_tiles),
        out_shape=(
            jax.ShapeDtypeStruct(displacement.shape, F32),
            jax.ShapeDtypeStruct((1, 128), F32),
        ),
        in_specs=[hbm, hbm, hbm],
        out_specs=(vmem, vmem),
        scratch_shapes=scratch,
        compiler_params=pltpu.CompilerParams(
            collective_id=0, has_side_effects=True, vmem_limit_bytes=64_000_000
        ),
    )(heights, displacement, rest_length)
    new_vel = velocity + 0.2 * forces
    return displacement + 0.05 * new_vel, new_vel, boost[0, 0]


def solution(mesh):
    tiled = P(None, "gx", "yz", None, None)
    sizes = (mesh.shape["gx"], mesh.shape["yz"])
    return jax.shard_map(
        functools.partial(body, *sizes),
        mesh=mesh,
        in_specs=(tiled, tiled, tiled, P()),
        out_specs=(tiled, tiled, P()),
        check_vma=False,
    )
```

```python
import functools

import jax
import jax.numpy as jnp
from jax import lax
from jax.experimental import pallas as pl
from jax.experimental.pallas import tpu as pltpu
from jax.sharding import PartitionSpec as P

CUTOFF_SQ = 1.5 * 1.5
REACH_SQ = 3.5 * 3.5
F32 = jnp.float32
MESH = pl.DeviceIdType.MESH


def list_offsets(reach_sq, forward_only):
    chosen = []
    for ax in range(-3, 4):
        for ay in range(-3, 4):
            for az in range(-3, 4):
                length_sq = ax * ax + ay * ay + az * az
                if 0 < length_sq <= reach_sq:
                    if not forward_only or (ax, ay, az) > (0, 0, 0):
                        chosen.append((ax, ay, az))
    return chosen


FORWARD = list_offsets(2, True)
BONDS = FORWARD + [(-v[0], -v[1], -v[2]) for v in FORWARD]
REACH = list_offsets(9, False)
ROUNDS = [(3, 0, 3), (1, 3, 3), (1, 4, 3), (1, 5, 1), (2, 6, 1)]


def kernel(n_gx, n_yz, z_tiles, heights_hbm, disp, rest_hbm, forces, boost, *scratch):
    xr, yr, zr, ys, zs = (scratch[i:25:5] for i in range(5))
    (store, zb, hb, ins, bonds, part, first, sums, send_sem, recv_sem, red_send, red_recv, rest, heights, load_sem) = scratch[25:]
    nx_all, ny_all = heights.shape
    loads = [
        pltpu.make_async_copy(heights_hbm, heights, load_sem.at[0]),
        pltpu.make_async_copy(disp.at[:, :, 0], xr[0].at[0], load_sem.at[1]),
        pltpu.make_async_copy(rest_hbm, rest, load_sem.at[2]),
    ]
    for load in loads:
        load.start()
    planes, rows, cols = disp.shape[1], disp.shape[3], disp.shape[4]
    y_tiles = n_yz // z_tiles
    gx = lax.axis_index("gx")
    me = lax.axis_index("yz")
    h = me + z_tiles // 2
    y_tile = lax.rem(h // z_tiles, y_tiles)
    z_tile = lax.rem(h, z_tiles)
    x_steps = [0, 1] if n_gx == 2 else [0, 1, -1]
    n_slots = len(x_steps)
    steps = [0, 1, -1]

    def target(a, b, c):
        to_y = lax.rem(y_tile + b + y_tiles, y_tiles)
        to_z = lax.rem(z_tile + c + z_tiles, z_tiles)
        to = lax.rem(to_y * z_tiles + to_z + n_yz - z_tiles // 2, n_yz)
        return (lax.rem(gx + a + n_gx, n_gx), to)

    n_dev = n_gx * n_yz
    rank = gx * n_yz + me
    barrier = pltpu.get_barrier_semaphore()

    def greet(k, carry):
        to = lax.rem(rank + k, n_dev)
        pl.semaphore_signal(barrier, inc=1, device_id=(to // n_yz, lax.rem(to, n_yz)), device_id_type=MESH)
        return carry

    lax.fori_loop(1, n_dev, greet, 0)

    lane = lax.broadcasted_iota(jnp.int32, (8, 128), 1)

    left_slot = 1
    right_slot = n_slots - 1
    last_tile = z_tile == z_tiles - 1
    first_tile = z_tile == 0

    def messages(r):
        halo = ROUNDS[r][2]
        out = []
        if halo == 1:
            edge = planes - 1
            out.append((xr[r].at[0, :, edge], xr[r].at[left_slot, :, edge], 1, 0, 0))
            out.append((xr[r].at[0, :, 0], xr[r].at[right_slot, :, 0], -1, 0, 0))
        else:
            for ai in range(1, n_slots):
                out.append((xr[r].at[0], xr[r].at[ai], x_steps[ai], 0, 0))
        for ai, a in reversed(list(enumerate(x_steps))):
            for bi in range(2):
                out.append((ys[r].at[bi], yr[r].at[bi, ai], a, steps[1 + bi], 0))
        for ci in range(2):
            for ai, a in enumerate(x_steps):
                for bi in range(2):
                    out.append((zs[r].at[ci, 1 - bi], zr[r].at[ci, ai, 2 + bi], a, steps[1 + bi], steps[1 + ci]))
                out.append((zs[r].at[ci], zr[r].at[ci, ai, 0:2], a, 0, steps[1 + ci]))
        return [
            (
                c,
                pltpu.make_async_remote_copy(
                    src_ref=src,
                    dst_ref=dst,
                    send_sem=send_sem.at[r, i],
                    recv_sem=recv_sem.at[r, i],
                    device_id=target(a, b, c),
                    device_id_type=MESH,
                ),
            )
            for i, (src, dst, a, b, c) in enumerate(out)
        ]

    def along(r, step, act, sending):
        chosen = [copy for c, copy in messages(r) if c == step]
        edge = last_tile if (step > 0) == sending else first_tile
        if step == 0:
            for copy in chosen:
                act(copy)
        else:

            @pl.when(jnp.logical_not(edge))
            def _():
                for copy in chosen:
                    act(copy)

    def pack(r):
        count, _, halo = ROUNDS[r]
        up = jnp.zeros((8, 128), F32)
        down = jnp.zeros((8, 128), F32)
        for q in range(count):
            for p in range(planes):
                item = q * planes + p
                low = xr[r][0, q, p, :, 0:128]
                high = xr[r][0, q, p, :, cols - 128 : cols]
                here = (lane >= 4 * item) & (lane < 4 * item + 4)
                up = jnp.where(here, pltpu.roll(high, (4 * item + 4) % 128, 1), up)
                down = jnp.where(here, pltpu.roll(low, (4 * item) % 128, 1), down)
                for half in range(2):
                    at = ((q * 2 + half) * planes + p) * halo
                    span = slice(half * 128, half * 128 + 128)
                    ys[r][0, at : at + halo] = xr[r][0, q, p, rows - halo : rows, span]
                    ys[r][1, at : at + halo] = xr[r][0, q, p, 0:halo, span]
        zs[r][0, 0], zs[r][0, 1] = up[0:4], up[4:8]
        zs[r][1, 0], zs[r][1, 1] = down[0:4], down[4:8]

    def send(r):
        if r:
            pack(r)
        for step in steps:
            along(r, step, lambda copy: copy.start(), True)

    def receive(r):
        for step in steps:
            along(r, step, lambda copy: copy.wait_recv(), False)
        count, base, halo = ROUNDS[r]
        for ci in range(2):
            edge = first_tile if ci == 0 else last_tile

            @pl.when(edge)
            def _():
                for ai in range(n_slots):
                    zb[ai, ci] = jnp.zeros((16, 128), F32)

            @pl.when(jnp.logical_not(edge))
            def _():
                for ai in range(n_slots):
                    zb[ai, ci, 0:4] = zr[r][ci, ai, 2]
                    zb[ai, ci, 4:8] = zr[r][ci, ai, 0]
                    zb[ai, ci, 8:12] = zr[r][ci, ai, 1]
                    zb[ai, ci, 12:16] = zr[r][ci, ai, 3]

        def one(xp, carry):
            plane = (xp - 3) % planes
            slot = left_slot if xp < 3 else 0 if xp < 3 + planes else right_slot
            for q in range(count):
                for half in range(2):
                    span = slice(half * 128, half * 128 + 128)
                    store[base + q, 3, half, xp, 4:12] = xr[r][slot, q, plane, :, span]
                    at = ((q * 2 + half) * planes + plane) * halo
                    store[base + q, 3, half, xp, 4 - halo : 4] = yr[r][0, slot, pl.ds(at, halo)]
                    store[base + q, 3, half, xp, 12 : 12 + halo] = yr[r][1, slot, pl.ds(at, halo)]
            for q in range(count):
                item = q * planes + plane
                for rt in range(2):
                    band = slice(8 * rt, 8 * rt + 8)
                    t1 = store[base + q, 3, 0, xp, band]
                    t2 = store[base + q, 3, 1, xp, band]
                    below = zb[slot, 0, band]
                    above = zb[slot, 1, band]
                    for dz in range(1, halo + 1):
                        r0 = pltpu.roll(below, (124 - 4 * item + dz) % 128, 1)
                        r1 = pltpu.roll(t1, dz, 1)
                        r2 = pltpu.roll(t2, dz, 1)
                        store[base + q, 3 - dz, 0, xp, band] = jnp.where(lane < dz, r0, r1)
                        store[base + q, 3 - dz, 1, xp, band] = jnp.where(lane < dz, r1, r2)
                        s1 = pltpu.roll(t1, 128 - dz, 1)
                        s2 = pltpu.roll(t2, 128 - dz, 1)
                        s3 = pltpu.roll(above, (-4 * item - dz) % 128, 1)
                        store[base + q, 3 + dz, 0, xp, band] = jnp.where(lane >= 128 - dz, s2, s1)
                        store[base + q, 3 + dz, 1, xp, band] = jnp.where(lane >= 128 - dz, s3, s2)
            return carry

        for xp in range(3 - halo, 3 + planes + halo):
            one(xp, 0)

    def far(q, x, half, d):
        return store[q, d[2] + 3, half, x + 3 + d[0], 4 + d[1] : 12 + d[1]]

    def separation(x, half, d, mine):
        pieces = []
        for c in range(3):
            delta = far(c, x, half, d) - mine[c]
            pieces.append(delta + float(d[c]) if d[c] else delta)
        return pieces

    def own(q, x, half):
        return far(q, x, half, (0, 0, 0))

    def put(ref, q, x, half, value):
        ref[0, q, x, :, half * 128 : half * 128 + 128] = value

    def tiles(body):
        def step(x, carry):
            for half in range(2):
                body(2 * x + half, x, half)
            return carry

        lax.fori_loop(0, planes, step, 0)

    loads[0].wait()

    def height_row(xp, carry):
        at_x = lax.rem(gx * planes + xp - 3 + nx_all, nx_all)
        for row in range(3, 13):
            at_y = lax.rem(y_tile * rows + row - 4 + ny_all, ny_all)
            hb[xp, row : row + 1] = jnp.full((1, 128), heights[at_x, at_y], jnp.int32)
        return carry

    lax.fori_loop(2, 4 + planes, height_row, 0)
    loads[1].wait()
    pack(0)
    pl.semaphore_wait(barrier, n_dev - 1)
    send(0)

    def count_column(i, carry):
        for j in range(ny_all):
            carry = carry + jnp.clip(heights[i, j], 0, z_tiles * cols)
        return carry

    atoms = lax.fori_loop(0, nx_all, count_column, jnp.zeros((), jnp.int32))
    loads[2].wait()
    receive(0)

    def bond_pass(i, x, half):
        mine = [own(c, x, half) for c in range(3)]
        layer = lane + (z_tile * cols + half * 128)
        here = layer < hb[x + 3, 4:12]
        density = jnp.zeros((8, 128), F32)
        energy = jnp.zeros((8, 128), F32)
        room = jnp.zeros((8, 128), F32)
        for k, d in enumerate(BONDS):
            s = separation(x, half, d, mine)
            r_sq = s[0] * s[0] + s[1] * s[1] + s[2] * s[2]
            inv_r = lax.rsqrt(r_sq)
            radius = r_sq * inv_r
            partner = layer + d[2] < hb[x + 3 + d[0], 4 + d[1] : 12 + d[1]]
            if d[2] < 0:
                partner = partner & (layer >= -d[2])
            paired = partner & here
            decay = jnp.exp(3.0 - 3.0 * radius)
            cut = jnp.maximum(1.0 - r_sq * (1.0 / CUTOFF_SQ), 0.0)
            cut_value = cut * cut
            length = rest_half(k, x, half)
            gain = 10.0 / length
            strain = (radius - length) * gain
            squared = strain * strain
            lifted = jnp.exp(8.0 * squared)
            density = density + jnp.where(partner, decay * cut_value, 0.0)
            energy = energy + jnp.where(paired, lifted, 0.0)
            room = room + jnp.where(paired, 1.0 - squared, 0.0)
            scale = jnp.where(paired, inv_r, 0.0)
            cut_slope = (-4.0 / CUTOFF_SQ) * radius * cut
            bonds[i, k, 0] = scale * 0.6 * (decay * decay) * (cut_slope - 6.0 * cut_value)
            bonds[i, k, 1] = scale * decay * (cut_slope - 3.0 * cut_value)
            strain_slope = scale * (2.0 * strain * gain)
            bonds[i, k, 2] = strain_slope * (8.0 * lifted)
            bonds[i, k, 3] = strain_slope
        put(xr[1], 0, x, half, energy)
        put(xr[4], 0, x, half, -0.5 * lax.rsqrt(density + 0.5))
        part[i, 0] = room

    def rest_half(k, x, half):
        return rest[k, x, 0, :, slice(half * 128, half * 128 + 128)]

    tiles(bond_pass)
    send(1)

    def reach_pass(i, x, half):
        mine = [own(c, x, half) for c in range(3)]
        for k, d in enumerate(REACH):
            s = separation(x, half, d, mine)
            r_sq = s[0] * s[0] + s[1] * s[1] + s[2] * s[2]
            ins[i, k] = jnp.maximum(1.0 - r_sq * (1.0 / REACH_SQ), 0.0)

    tiles(reach_pass)
    receive(1)
    first[...] = jnp.zeros_like(first)

    def tapered(q, i, x, half):
        sums_of = [jnp.zeros((8, 128), F32) for _ in range(4)]
        for k, d in enumerate(REACH):
            inside = ins[i, k]
            sums_of[k % 4] = sums_of[k % 4] + (inside * inside) * far(q, x, half, d)
        return (sums_of[0] + sums_of[1]) + (sums_of[2] + sums_of[3])

    def smooth_pass(i, x, half):
        energy = own(3, x, half)
        total = 1.0 + energy + tapered(3, i, x, half)
        room = part[i, 0]
        smooth = jnp.log(total) * 0.125
        share = 1.0 / (1.0 + smooth * smooth)
        gain = 0.08 * share
        layer = lane + (z_tile * cols + half * 128)
        here = layer < hb[x + 3, 4:12]
        adjoint = room * 0.08 * (-2.0 * smooth) * (share * share) / (8.0 * total)
        put(xr[2], 0, x, half, jnp.where(here, adjoint, 0.0))
        put(xr[4], 1, x, half, gain)
        first[...] += jnp.where(here, jnp.exp(gain * room * 2.0), 0.0)

    tiles(smooth_pass)
    send(2)
    send(4)
    sums[0] = jnp.sum(first[...], axis=0, keepdims=True)

    def reduction(k):
        to = lax.rem(rank + k, n_dev)
        return pltpu.make_async_remote_copy(
            src_ref=sums.at[0],
            dst_ref=sums.at[k],
            send_sem=red_send.at[k],
            recv_sem=red_recv.at[k],
            device_id=(to // n_yz, lax.rem(to, n_yz)),
            device_id_type=MESH,
        )

    def spread(k, carry):
        reduction(k).start()
        return carry

    lax.fori_loop(1, n_dev, spread, 0)

    def pull(source):
        def run(i, x, half):
            mine = [own(c, x, half) for c in range(3)]
            total = [jnp.zeros((8, 128), F32) for _ in range(3)]
            for k, d in enumerate(REACH):
                s = separation(x, half, d, mine)
                weight = ins[i, k] * far(source, x, half, d)
                total = [total[c] + weight * s[c] for c in range(3)]
            return total

        return run

    def energy_pull(i, x, half):
        total = pull(3)(i, x, half)
        for c in range(3):
            part[i, 1 + c] = total[c]

    tiles(energy_pull)
    receive(2)

    def lambda_pass(i, x, half):
        put(xr[3], 0, x, half, own(4, x, half) + tapered(4, i, x, half))

    tiles(lambda_pass)
    send(3)

    def adjoint_pull(i, x, half):
        total = pull(4)(i, x, half)
        adjoint = own(4, x, half)
        energy = own(3, x, half)
        for c in range(3):
            part[i, 1 + c] = (-4.0 / REACH_SQ) * (adjoint * part[i, 1 + c] + energy * total[c])

    tiles(adjoint_pull)
    receive(4)

    def final_pass(i, x, half):
        mine = [own(c, x, half) for c in range(3)]
        lam, embed, gain = own(5, x, half), own(6, x, half), own(7, x, half)
        force = [part[i, 1 + c] for c in range(3)]
        for k, d in enumerate(BONDS):
            s = separation(x, half, d, mine)
            weight = (
                bonds[i, k, 0]
                + (embed + far(6, x, half, d)) * bonds[i, k, 1]
                + (lam + far(5, x, half, d)) * bonds[i, k, 2]
                - (gain + far(7, x, half, d)) * bonds[i, k, 3]
            )
            force = [force[c] + weight * s[c] for c in range(3)]
        span = slice(half * 128, half * 128 + 128)
        for c in range(3):
            forces[c, x, 0, :, span] = force[c]

    def collect(k, carry):
        reduction(k).wait_recv()
        return carry

    lax.fori_loop(1, n_dev, collect, 0)
    total = jnp.sum(jnp.sum(sums[...], axis=0), axis=1, keepdims=True)
    boost[...] = jnp.broadcast_to(total, (1, 128)) / jnp.full((1, 128), atoms.astype(F32))

    receive(3)
    tiles(final_pass)

    def finish(k, carry):
        reduction(k).wait_send()
        return carry

    lax.fori_loop(1, n_dev, finish, 0)
    for r in range(5):
        for step in steps:
            along(r, step, lambda copy: copy.wait_send(), True)


def body(n_gx, n_yz, displacement, velocity, rest_length, heights):
    _, planes, _, rows, cols = displacement.shape
    z_tiles = n_yz // (heights.shape[1] // rows)
    slots = 2 if n_gx == 2 else 3
    n_dev = n_gx * n_yz
    n_msg = 2 + 2 * slots + 6 * slots
    scratch = []
    for count, _, halo in ROUNDS:
        y_rows = count * 2 * planes * halo
        scratch += [
            pltpu.VMEM((slots, count, planes, rows, cols), F32),
            pltpu.VMEM((2, slots, y_rows, 128), F32),
            pltpu.VMEM((2, slots, 4, 4, 128), F32),
            pltpu.VMEM((2, y_rows, 128), F32),
            pltpu.VMEM((2, 2, 4, 128), F32),
        ]
    scratch += [
        pltpu.VMEM((8, 7, 2, planes + 6, 16, 128), F32),
        pltpu.VMEM((slots, 2, 16, 128), F32),
        pltpu.VMEM((planes + 6, 16, 128), jnp.int32),
        pltpu.VMEM((2 * planes, len(REACH), 8, 128), F32),
        pltpu.VMEM((2 * planes, len(BONDS), 4, 8, 128), F32),
        pltpu.VMEM((2 * planes, 4, 8, 128), F32),
        pltpu.VMEM((8, 128), F32),
        pltpu.VMEM((n_dev, 1, 128), F32),
        pltpu.SemaphoreType.DMA((len(ROUNDS), n_msg)),
        pltpu.SemaphoreType.DMA((len(ROUNDS), n_msg)),
        pltpu.SemaphoreType.DMA((n_dev,)),
        pltpu.SemaphoreType.DMA((n_dev,)),
        pltpu.VMEM(rest_length.shape, F32),
        pltpu.SMEM(heights.shape, jnp.int32),
        pltpu.SemaphoreType.DMA((3,)),
    ]
    vmem = pl.BlockSpec(memory_space=pltpu.VMEM)
    hbm = pl.BlockSpec(memory_space=pltpu.HBM)
    forces, boost = pl.pallas_call(
        functools.partial(kernel, n_gx, n_yz, z_tiles),
        out_shape=(
            jax.ShapeDtypeStruct(displacement.shape, F32),
            jax.ShapeDtypeStruct((1, 128), F32),
        ),
        in_specs=[hbm, hbm, hbm],
        out_specs=(vmem, vmem),
        scratch_shapes=scratch,
        compiler_params=pltpu.CompilerParams(
            collective_id=0, has_side_effects=True, vmem_limit_bytes=64_000_000
        ),
    )(heights, displacement, rest_length)
    new_vel = velocity + 0.2 * forces
    return displacement + 0.05 * new_vel, new_vel, boost[0, 0]


def solution(mesh):
    tiled = P(None, "gx", "yz", None, None)
    sizes = (mesh.shape["gx"], mesh.shape["yz"])
    return jax.shard_map(
        functools.partial(body, *sizes),
        mesh=mesh,
        in_specs=(tiled, tiled, tiled, P()),
        out_specs=(tiled, tiled, P()),
        check_vma=False,
    )
```
